32 devices in a mesh: section: 2 (over core), dp: 4 (over z), mp: 4 (over y, x).
Axes of the slice: x: 2, y: 2, z: 4, core: 2. Of those that a mesh axis runs over, the one named last changes fastest.
Arguments:
- boundary: bfloat16 [2, 2, 4096, 1024], P('section', None, ('dp', 'mp')), may hold values from -6 to 6
- pieces: int32 [2, 4], P(None, 'dp'), may hold values from 1 to 2, as said below
- attn_gain: bfloat16 [2, 1024], P('section'), may hold values from 0.5 to 1.5
- w_query: bfloat16 [2, 1024, 1024], P('section', 'mp'), may hold values from -0.1875 to 0.1875
- w_key: bfloat16 [2, 1024, 1024], P('section', 'mp'), may hold values from -0.1875 to 0.1875
- w_value: bfloat16 [2, 1024, 1024], P('section', 'mp'), may hold values from -0.1875 to 0.1875
- w_out: bfloat16 [2, 1024, 1024], P('section', 'mp'), may hold values from -2 to 2
- ffn_gain: bfloat16 [2, 1024], P('section'), may hold values from 0.5 to 1.5
- w_gate: bfloat16 [2, 2816, 1024], P('section', 'mp'), may hold values from -0.1875 to 0.1875
- w_up: bfloat16 [2, 2816, 1024], P('section', 'mp'), may hold values from -0.1875 to 0.1875
- w_down: bfloat16 [2, 2816, 1024], P('section', 'mp'), may hold values from -0.109375 to 0.109375
Outputs:
- ends: float32 [2, 2, 4096, 1024], P('section', None, ('dp', 'mp'))
- g_attn_gain: float32 [2, 1024], P('section')
- g_w_query: float32 [2, 1024, 1024], P('section', 'mp')
- g_w_key: float32 [2, 1024, 1024], P('section', 'mp')
- g_w_value: float32 [2, 1024, 1024], P('section', 'mp')
- g_w_out: float32 [2, 1024, 1024], P('section', 'mp')
- g_ffn_gain: float32 [2, 1024], P('section')
- g_w_gate: float32 [2, 2816, 1024], P('section', 'mp')
- g_w_up: float32 [2, 2816, 1024], P('section', 'mp')
- g_w_down: float32 [2, 2816, 1024], P('section', 'mp')
The draws below stay inside these ranges and needn't reach their ends.
Inputs may be any that keep to these rules, and one draw needn't show every extreme that they name: The rows of one micro-batch on one index of dp hold pieces equal sequences; both 1 and 2 occur in every draw.
All inputs are finite; a program needn't handle non-finite values.
Results may differ from the reference program's by a relative error of at most 0.035.
Values may be sent and summed in bfloat16 or wider, within the bound.
No kernel may reach another device: no remote copies, remote signals or barrier semaphores. Data moves between devices by JAX's collectives and lax.ppermute only.
A program may use at most 256 MiB of HBM per device.

```python
import math
import jax
import jax.numpy as jnp
from jax import lax

D = 1024
HEADS = 16
HD = 64
FF = 2816
ROWS = 1024
MB = 2
QW = 1024
TOKENS = 4096


def draw_pieces(key, part):
    total_count = MB * (TOKENS // ROWS)
    draw_key, spot_key, offset_key = jax.random.split(key, 3)
    drawn = jax.random.randint(draw_key, (total_count,), 1, 3)
    high_spot = jax.random.randint(spot_key, (), 0, total_count)
    offset = jax.random.randint(offset_key, (), 1, total_count)
    drawn = drawn.at[high_spot].set(2)
    drawn = drawn.at[(high_spot + offset) % total_count].set(1)
    return drawn.reshape(MB, TOKENS // ROWS).astype(jnp.int32)


def shard_levels(rng, extent, cuts, smallest, largest):
    gain, own = 1.0, jax.random.fold_in(rng, 6)
    for dim, shards_of in cuts:
        heights = jnp.exp(jax.random.uniform(jax.random.fold_in(own, dim), (shards_of,), jnp.float32, smallest / len(cuts), largest / len(cuts)))
        gain = gain * jnp.repeat(heights, extent[dim] // shards_of).reshape([-1 if axis == dim else 1 for axis in range(len(extent))])
    return gain


def bell_draw(key, dims, scale, reach, shards=(), kind=jnp.bfloat16):
    entries = scale * jax.random.normal(key, dims, jnp.float32)
    if shards:
        entries = entries * shard_levels(key, dims, shards, -0.22, 0.18)
    return jnp.clip(entries, -reach, reach).astype(kind)


def setup_inputs(seed: int = 0) -> dict:
    keys = jax.random.split(jax.random.key(seed), 12)
    boundary = bell_draw(keys[0], (2, MB, TOKENS, D), 1.0, 6.0, ((0, 2), (2, 16)))
    pieces = draw_pieces(jax.random.fold_in(keys[11], 71), 0)
    attn_gain = jnp.clip(1.0 + 0.1 * jax.random.normal(keys[2], (2, D), jnp.float32), 0.5, 1.5).astype(jnp.bfloat16)
    w_query = bell_draw(keys[3], (2, QW, D), D ** -0.5, 0.1875, ((0, 2), (1, 4)))
    w_key = bell_draw(keys[4], (2, QW, D), D ** -0.5, 0.1875, ((0, 2), (1, 4)))
    w_value = bell_draw(keys[5], (2, QW, D), D ** -0.5, 0.1875, ((0, 2), (1, 4)))
    w_out = bell_draw(keys[6], (2, QW, D), (max(1, 8 * QW // ROWS)) ** -0.5, 2.0, ((0, 2), (1, 4)))
    ffn_gain = jnp.clip(1.0 + 0.1 * jax.random.normal(keys[7], (2, D), jnp.float32), 0.5, 1.5).astype(jnp.bfloat16)
    w_gate = bell_draw(keys[8], (2, FF, D), D ** -0.5, 0.1875, ((0, 2), (1, 4)))
    w_up = bell_draw(keys[9], (2, FF, D), D ** -0.5, 0.1875, ((0, 2), (1, 4)))
    w_down = bell_draw(keys[10], (2, FF, D), FF ** -0.5, 0.109375, ((0, 2), (1, 4)))
    return {"boundary": boundary, "pieces": pieces, "attn_gain": attn_gain, "w_query": w_query, "w_key": w_key, "w_value": w_value, "w_out": w_out, "ffn_gain": ffn_gain, "w_gate": w_gate, "w_up": w_up, "w_down": w_down}


epsilon = 1e-06
precise = lax.Precision.HIGHEST

@jax.custom_vjp
def low(v):
    return lax.optimization_barrier(v.astype(jnp.bfloat16)).astype(jnp.float32)

@jax.custom_vjp
def low_back(v):
    return v

def low_keep(v):
    return (low(v), None)

def low_pass(kept, grad):
    return (grad,)

def back_keep(v):
    return (v, None)

def back_low(kept, grad):
    return (low(grad),)
low.defvjp(low_keep, low_pass)
low_back.defvjp(back_keep, back_low)

def rounded(tensor):
    return low_back(low(tensor))

def matmul(left_side, right_side):
    return jnp.dot(left_side, right_side, precision=precise, preferred_element_type=jnp.float32)

def normalize(hidden_in):
    return hidden_in * lax.rsqrt(lax.optimization_barrier(jnp.mean(hidden_in * hidden_in, axis=-1, keepdims=True)) + epsilon)

def layout(sequences):
    piece_length = ROWS // sequences
    row_index = jnp.arange(ROWS, dtype=jnp.int32)
    position = row_index % piece_length
    segment = row_index // piece_length
    half_size = HD // 2
    frequency = jnp.exp(-math.log(10000.0) * (2.0 * jnp.arange(half_size, dtype=jnp.float32)) / HD)
    turned = position.astype(jnp.float32)[:, None] * frequency[None, :]
    return (jnp.cos(turned)[:, None, :], jnp.sin(turned)[:, None, :], position, segment)

def rotate(tensor, cosines, sine_values):
    half_size = tensor.shape[-1] // 2
    former = tensor[..., :half_size]
    latter = tensor[..., half_size:]
    return jnp.concatenate([former * cosines - latter * sine_values, latter * cosines + former * sine_values], axis=-1)

def attention(queries, keys_all, values_all, position, segment):
    block_rows = min(512, ROWS)
    block_count = ROWS // block_rows
    blocked = (queries.reshape(block_count, block_rows, HEADS, HD), position.reshape(block_count, block_rows), segment.reshape(block_count, block_rows))

    def one_block(inputs):
        query_part, place_part, segment_part = inputs
        scores = jnp.einsum('qhd,khd->hqk', query_part, keys_all, precision=precise) * 0.125
        scores = low_back(scores)
        allowed = (segment_part[:, None] == segment[None, :]) & (position[None, :] <= place_part[:, None])
        scores = jnp.where(allowed[None], scores, -1e+30)
        weights = jax.nn.softmax(scores, axis=-1)
        return jnp.einsum('hqk,khd->qhd', low(weights), values_all, precision=precise)
    output = lax.map(jax.checkpoint(one_block), blocked)
    return output.reshape(ROWS, HEADS * HD)

def layer(hidden_in, params, cosines, sine_values, position, segment, first_values):
    attn_gain, w_query, w_key, w_value, w_out, ffn_gain, w_gate, w_up, w_down = params
    normed = low(normalize(hidden_in) * attn_gain)
    queries = rounded(rotate(low_back(matmul(normed, w_query.T)).reshape(ROWS, HEADS, HD), cosines, sine_values))
    keys_all = rounded(rotate(low_back(matmul(normed, w_key.T)).reshape(ROWS, HEADS, HD), cosines, sine_values))
    values_raw = matmul(normed, w_value.T)
    if first_values is None:
        values_all = rounded(values_raw)
    else:
        values_all = rounded(0.5 * values_raw + 0.5 * first_values)
    attended = rounded(attention(queries, keys_all, values_all.reshape(ROWS, HEADS, HD), position, segment))
    mixed_rows = hidden_in + low_back(matmul(attended, w_out))
    normed_ffn = low(normalize(mixed_rows) * ffn_gain)
    gate_proj = low_back(matmul(normed_ffn, w_gate.T))
    up_proj = low_back(matmul(normed_ffn, w_up.T))
    activated = low(jax.nn.silu(gate_proj) * up_proj)
    result = mixed_rows + low_back(matmul(activated, w_down))
    return (result, values_all)

def network(params, given_rows, sequences):
    cosines, sine_values, position, segment = layout(sequences)
    first_params = tuple((tensor[0] for tensor in params))
    second_params = tuple((tensor[1] for tensor in params))
    hidden_one, first_values = layer(given_rows, first_params, cosines, sine_values, position, segment, None)
    hidden_one = rounded(hidden_one)
    output, unused_values = layer(hidden_one, second_params, cosines, sine_values, position, segment, first_values)
    return output

def reference(boundary, pieces, attn_gain, w_query, w_key, w_value, w_out, ffn_gain, w_gate, w_up, w_down):
    params = tuple((tensor.astype(jnp.float32) for tensor in (attn_gain, w_query, w_key, w_value, w_out, ffn_gain, w_gate, w_up, w_down)))
    buffers = MB * (TOKENS // ROWS)
    inputs = boundary[0].astype(jnp.float32).reshape(buffers, ROWS, D)
    cotangent = boundary[1].astype(jnp.float32).reshape(buffers, ROWS, D)
    counts = pieces.reshape(buffers).astype(jnp.int32)

    def one_buffer(totals, item):
        given_rows, upstream, sequences = item
        output, pullback = jax.vjp(lambda weights, start_rows: network(weights, start_rows, sequences), params, given_rows)
        grad_weights, grad_input = pullback(upstream)
        totals = jax.tree.map(lambda total_now, added: total_now + added, totals, grad_weights)
        return (totals, (output, grad_input))
    zero_totals = jax.tree.map(jnp.zeros_like, params)
    totals, (outputs, grads_in) = lax.scan(one_buffer, zero_totals, (inputs, cotangent, counts))
    ends = jnp.stack([grads_in.reshape(MB, TOKENS, D), outputs.reshape(MB, TOKENS, D)])
    return (ends, totals[0], totals[1], totals[2], totals[3], totals[4], totals[5], totals[6], totals[7], totals[8])
```

```python
import math

import jax
import jax.numpy as jnp
from jax import lax
from jax.sharding import PartitionSpec as P

HD = 64
epsilon = 1e-06
f32, bf16 = jnp.float32, jnp.bfloat16


def normalize(hidden_in):
    scale_rows = lax.rsqrt(jnp.mean(hidden_in * hidden_in, axis=-1, keepdims=True) + epsilon)
    return (hidden_in * scale_rows, scale_rows)


def norm_back(upstream, unit_rows, scale_rows, weight_gain):
    scaled = upstream * weight_gain
    return scale_rows * (scaled - unit_rows * jnp.mean(scaled * unit_rows, axis=-1, keepdims=True))


def layout(row_index, total_rows, head_size, sequences):
    piece_length = total_rows // sequences
    position = row_index % piece_length
    segment = row_index // piece_length
    half_size = head_size // 2
    frequency = jnp.exp(
        -math.log(10000.0) * (2.0 * jnp.arange(half_size, dtype=jnp.float32)) / head_size
    )
    turned = position.astype(jnp.float32)[:, None] * frequency[None, :]
    return (jnp.cos(turned)[:, None, :], jnp.sin(turned)[:, None, :], position, segment)


def rotate(tensor, cosines, sine_values):
    half_size = tensor.shape[-1] // 2
    former = tensor[..., :half_size]
    latter = tensor[..., half_size:]
    return jnp.concatenate(
        [former * cosines - latter * sine_values, latter * cosines + former * sine_values], axis=-1
    )


def rotate_back(tensor, cosines, sine_values):
    return rotate(tensor, cosines, -sine_values)


def contract_rows(left_side, right_side):
    return lax.dot_general(
        left_side, right_side, (((0,), (0,)), ((), ())), preferred_element_type=jnp.float32
    )


def times_transposed(left_side, right_side):
    return lax.dot_general(
        left_side, right_side, (((1,), (1,)), ((), ())), preferred_element_type=jnp.float32
    )


def times(left_side, right_side):
    return jnp.dot(left_side, right_side, preferred_element_type=jnp.float32)


def allowed_mask(place_part, segment_part, position, segment):
    return (segment_part[:, None] == segment[None, :]) & (position[None, :] <= place_part[:, None])


def attend(queries, keys_all, values_all, position, segment, block_rows):
    total_rows, heads_here, head_size = queries.shape
    block_count = total_rows // block_rows
    blocked = (
        queries.reshape(block_count, block_rows, heads_here, head_size),
        position.reshape(block_count, block_rows),
        segment.reshape(block_count, block_rows),
    )

    def one_block(inputs):
        query_part, place_part, segment_part = inputs
        scores = (
            jnp.einsum("qhd,khd->hqk", query_part, keys_all, preferred_element_type=jnp.float32)
            * 0.125
        )
        scores = jnp.where(
            allowed_mask(place_part, segment_part, position, segment)[None], scores, -1e30
        )
        highest = jnp.max(scores, axis=-1, keepdims=True)
        exponent = jnp.exp(scores - highest)
        denominator = jnp.sum(exponent, axis=-1, keepdims=True)
        probs = exponent / denominator
        output = jnp.einsum(
            "hqk,khd->qhd",
            probs.astype(jnp.bfloat16),
            values_all,
            preferred_element_type=jnp.float32,
        )
        return (output.astype(jnp.bfloat16), (highest + jnp.log(denominator))[..., 0])

    outputs, logsums = lax.map(one_block, blocked)
    return (outputs.reshape(total_rows, heads_here * head_size), logsums)


def attend_back(queries, keys_all, values_all, grad_out, logsums, position, segment, block_rows):
    total_rows, heads_here, head_size = queries.shape
    block_count = total_rows // block_rows
    blocked = (
        queries.reshape(block_count, block_rows, heads_here, head_size),
        grad_out.reshape(block_count, block_rows, heads_here, head_size),
        logsums,
        position.reshape(block_count, block_rows),
        segment.reshape(block_count, block_rows),
    )

    def one_block(carry, inputs):
        grad_keys, grad_values = carry
        query_part, grad_part, logsum_part, place_part, segment_part = inputs
        scores = (
            jnp.einsum("qhd,khd->hqk", query_part, keys_all, preferred_element_type=jnp.float32)
            * 0.125
        )
        allowed = allowed_mask(place_part, segment_part, position, segment)[None]
        scores = jnp.where(allowed, scores, -1e30)
        probs = jnp.where(allowed, jnp.exp(scores - logsum_part[..., None]), 0.0)
        grad_probs = jnp.einsum(
            "qhd,khd->hqk", grad_part, values_all, preferred_element_type=jnp.float32
        )
        centre = jnp.sum(grad_probs * probs, axis=-1, keepdims=True)
        grad_scores = (probs * (grad_probs - centre)).astype(jnp.bfloat16)
        grad_query = (
            jnp.einsum("hqk,khd->qhd", grad_scores, keys_all, preferred_element_type=jnp.float32)
            * 0.125
        )
        grad_keys = (
            grad_keys
            + jnp.einsum(
                "hqk,qhd->khd", grad_scores, query_part, preferred_element_type=jnp.float32
            )
            * 0.125
        )
        grad_values = grad_values + jnp.einsum(
            "hqk,qhd->khd",
            probs.astype(jnp.bfloat16),
            grad_part,
            preferred_element_type=jnp.float32,
        )
        return ((grad_keys, grad_values), grad_query)

    zero_rows = jnp.zeros((total_rows, heads_here, head_size), jnp.float32)
    (grad_keys, grad_values), grad_query = lax.scan(one_block, (zero_rows, zero_rows), blocked)
    return (grad_query.reshape(total_rows, heads_here, head_size), grad_keys, grad_values)


def add_low(left_side, right_side):
    return (left_side.astype(f32) + right_side.astype(f32)).astype(bf16)


NEAR, SIDE = [(0, 1), (1, 0), (2, 3), (3, 2)], [(0, 2), (2, 0), (1, 3), (3, 1)]
BLOCKS = 4


def to_near(block):
    return lax.ppermute(block, "mp", NEAR)


def to_side(block):
    return lax.ppermute(block, "mp", SIDE)


def square():
    return lax.axis_size("mp") == 4


def gather_blocks(block):
    if not square():
        whole = lax.all_gather(block, "mp", axis=0, tiled=True)
        return jnp.split(whole, BLOCKS, axis=0)
    half = block.shape[0] // 2
    near, side = to_near(block), to_side(block)
    far_top = to_near(side[:half])
    far_low = to_side(near[half:])
    return [block, near, side, jnp.concatenate([far_top, far_low])]


def scatter_blocks(partial_of):
    if not square():
        whole = jnp.concatenate([partial_of(j).astype(bf16) for j in range(BLOCKS)])
        return lax.psum_scatter(whole, "mp", scatter_dimension=0, tiled=True).astype(f32)
    far = partial_of(3).astype(bf16)
    half = far.shape[0] // 2
    far_top, far_low = to_near(far[:half]), to_side(far[half:])
    near, side = partial_of(1), partial_of(2)
    near = jnp.concatenate([near[:half], near[half:] + far_low.astype(f32)]).astype(bf16)
    side = jnp.concatenate([side[:half] + far_top.astype(f32), side[half:]]).astype(bf16)
    near, side = to_near(near), to_side(side)
    return partial_of(0) + near.astype(f32) + side.astype(f32)


def sum_line(block):
    if lax.axis_size("dp") != 4:
        return lax.psum(block, "dp")
    kind = block.dtype
    place = lax.axis_index("dp")
    middle = (place == 1) | (place == 2)
    from_end = lax.ppermute(block, "dp", [(0, 1), (3, 2)])
    pair = (block.astype(f32) + from_end.astype(f32)).astype(kind)
    across = lax.ppermute(pair, "dp", [(1, 2), (2, 1)])
    total = (pair.astype(f32) + across.astype(f32)).astype(kind)
    final = lax.ppermute(total, "dp", [(1, 0), (2, 3)])
    return jnp.where(middle, total, final)


def swap(block):
    return lax.ppermute(block, "section", [(0, 1), (1, 0)])


def after(value, *others):
    return lax.optimization_barrier((value, *others))[0]


def shards(
    boundary, pieces, attn_gain, w_query, w_key, w_value, w_out, ffn_gain, w_gate, w_up, w_down
):
    local_rows = boundary.shape[2]
    total_rows = local_rows * lax.axis_size("mp")
    block_rows = total_rows // BLOCKS
    head_size = HD
    local_width = w_query.shape[1]
    heads_here = local_width // head_size
    attend_rows = min(512, total_rows)
    section_index = lax.axis_index("section")
    is_first = section_index == 0
    is_last = section_index == 1

    def choose(first, second):
        return jnp.where(is_first, first, second)

    kept_rows = choose(boundary[0, 0], boundary[0, 1])
    sent_rows = choose(boundary[0, 1], boundary[0, 0])
    got_rows = swap(sent_rows)
    start_rows = choose(kept_rows, got_rows)
    cotangent = choose(got_rows, kept_rows)

    own = (
        jnp.stack([attn_gain[0], ffn_gain[0]]),
        jnp.concatenate([w_query[0], w_key[0], w_value[0]], axis=0),
        w_out[0],
        w_gate[0],
        w_up[0],
        w_down[0],
    )
    other = tuple(swap(tensor) for tensor in own)
    weights = [
        tuple(choose(a, b) for a, b in zip(own, other)),
        tuple(choose(b, a) for a, b in zip(own, other)),
    ]

    if square():
        mine = lax.axis_index("mp")
        row_index = jnp.concatenate(
            [(mine ^ j) * block_rows + jnp.arange(block_rows, dtype=jnp.int32) for j in range(4)]
        )
    else:
        row_index = jnp.arange(total_rows, dtype=jnp.int32)
    sequences = choose(pieces[0, 0], pieces[1, 0])
    cosines, sine_values, position, segment = layout(row_index, total_rows, head_size, sequences)

    def rows_of(tensor, j):
        return tensor[j * block_rows : (j + 1) * block_rows]

    def heads(tensor):
        return tensor.reshape(tensor.shape[0], heads_here, head_size)

    def flat(tensor):
        return tensor.reshape(tensor.shape[0], local_width)

    def forward(hidden_in, layer_weights, first_values):
        gains, joined, weight_out, weight_gate, weight_up, weight_down = layer_weights
        gains = gains.astype(f32)
        unit_rows, scale_rows = normalize(hidden_in)
        gathered = gather_blocks((unit_rows * gains[0]).astype(bf16))
        queries, keys_all, values_all = [], [], []
        for j in range(BLOCKS):
            projected = times_transposed(gathered[j], joined)
            turn = (rows_of(cosines, j), rows_of(sine_values, j))
            queries.append(rotate(heads(projected[:, :local_width]), *turn).astype(bf16))
            keys_all.append(
                rotate(heads(projected[:, local_width : 2 * local_width]), *turn).astype(bf16)
            )
            own_values = projected[:, 2 * local_width :]
            if first_values is not None:
                own_values = 0.5 * own_values + 0.5 * first_values[j].astype(f32)
            values_all.append(own_values.astype(bf16))
        q_all, k_all = jnp.concatenate(queries), jnp.concatenate(keys_all)
        v_all = heads(jnp.concatenate(values_all))
        attended, logsums = attend(q_all, k_all, v_all, position, segment, attend_rows)
        mixed_rows = hidden_in + scatter_blocks(
            lambda j: times(rows_of(attended, j), weight_out)
        )
        unit_ffn, scale_ffn = normalize(mixed_rows)
        gathered_ffn = gather_blocks((unit_ffn * gains[1]).astype(bf16))
        gates, ups, acts = [None] * BLOCKS, [None] * BLOCKS, [None] * BLOCKS

        def ffn_rows(j):
            gates[j] = times_transposed(gathered_ffn[j], weight_gate)
            ups[j] = times_transposed(gathered_ffn[j], weight_up)
            acts[j] = (jax.nn.silu(gates[j]) * ups[j]).astype(bf16)
            return times(acts[j], weight_down)

        result = mixed_rows + scatter_blocks(ffn_rows)
        kept = dict(
            unit_rows=unit_rows, scale_rows=scale_rows, gathered=gathered, q=q_all, k=k_all, v=v_all,
            attended=attended, logsums=logsums, unit_ffn=unit_ffn, scale_ffn=scale_ffn,
            gathered_ffn=gathered_ffn, gates=gates, ups=ups, acts=acts, values=values_all,
        )
        return result, kept

    def share(grad):
        half = grad.shape[0] // 2
        grad = grad.astype(bf16)
        got = swap(choose(grad[half:], grad[:half]))
        return sum_line(add_low(choose(grad[:half], grad[half:]), got))

    def backward(upstream, grad_rows, kept, layer_weights, later_values):
        gains, joined, weight_out, weight_gate, weight_up, weight_down = layer_weights
        gains = gains.astype(f32)
        grad_gates, grad_ups = [None] * BLOCKS, [None] * BLOCKS

        def ffn_back(j):
            grad_act = times_transposed(grad_rows[j], weight_down)
            gate, up = kept["gates"][j], kept["ups"][j]
            sigmoid_gate = jax.nn.sigmoid(gate)
            grad_gates[j] = (
                grad_act * up * sigmoid_gate * (1.0 + gate * (1.0 - sigmoid_gate))
            ).astype(bf16)
            grad_ups[j] = (grad_act * jax.nn.silu(gate)).astype(bf16)
            return times(grad_gates[j], weight_gate) + times(grad_ups[j], weight_up)

        grad_normed_ffn = scatter_blocks(ffn_back)
        rows_ffn = jnp.concatenate(kept["gathered_ffn"])
        shares = {}
        shares["down"] = share(
            contract_rows(jnp.concatenate(kept["acts"]), jnp.concatenate(grad_rows))
        )
        shares["gate"] = share(contract_rows(jnp.concatenate(grad_gates), rows_ffn))
        shares["up"] = share(contract_rows(jnp.concatenate(grad_ups), rows_ffn))
        grad_ffn_gain = jnp.sum(grad_normed_ffn * kept["unit_ffn"], axis=0)
        grad_mixed = upstream + norm_back(
            grad_normed_ffn, kept["unit_ffn"], kept["scale_ffn"], gains[1]
        )
        grad_z = gather_blocks(grad_mixed.astype(bf16))
        grad_attended = jnp.concatenate(
            [times_transposed(grad_z[j], weight_out).astype(bf16) for j in range(BLOCKS)]
        )
        shares["out"] = share(contract_rows(kept["attended"], jnp.concatenate(grad_z)))
        grad_query, grad_keys, grad_values = attend_back(
            kept["q"], kept["k"], kept["v"], heads(grad_attended), kept["logsums"],
            position, segment, attend_rows,
        )
        values_total = flat(grad_values)
        if later_values is not None:
            values_total = (values_total + later_values.astype(f32)).astype(bf16)
            half_values, raw_values = None, values_total
        else:
            half_values = (0.5 * values_total.astype(bf16).astype(f32)).astype(bf16)
            raw_values = half_values
        query_low = lax.optimization_barrier(grad_query.astype(bf16)).astype(f32)
        keys_low = lax.optimization_barrier(grad_keys.astype(bf16)).astype(f32)
        raw_queries = flat(rotate_back(query_low, cosines, sine_values).astype(bf16))
        raw_keys = flat(rotate_back(keys_low, cosines, sine_values).astype(bf16))
        grad_joined = jnp.concatenate([raw_queries, raw_keys, raw_values], axis=1)
        grad_normed = scatter_blocks(lambda j: times(rows_of(grad_joined, j), joined))
        shares["joined"] = share(contract_rows(grad_joined, jnp.concatenate(kept["gathered"])))
        grad_attn_gain = jnp.sum(grad_normed * kept["unit_rows"], axis=0)
        grad_input = grad_mixed + norm_back(
            grad_normed, kept["unit_rows"], kept["scale_rows"], gains[0]
        )
        return grad_input, half_values, shares, (grad_attn_gain, grad_ffn_gain)

    first_result, first_kept = forward(start_rows.astype(f32), weights[0], None)
    grad_rows = gather_blocks(after(cotangent, first_kept["q"]))
    hidden_one = first_result.astype(bf16).astype(f32)
    result, second_kept = forward(hidden_one, weights[1], first_kept["values"])
    got_result = swap(result)
    grad_one, half_values, second_shares, second_gains = backward(
        cotangent.astype(f32), grad_rows, second_kept, weights[1], None
    )
    grad_low = grad_one.astype(bf16)
    grad_input, unused, first_shares, first_gains = backward(
        grad_low.astype(f32), gather_blocks(grad_low), first_kept, weights[0], half_values
    )
    got_input = swap(grad_input)

    def finish(name):
        first, second = first_shares[name], second_shares[name]
        got = swap(choose(second, first))
        top = choose(first, got)
        low = choose(got, second)
        return jnp.concatenate([top, low]).astype(f32)

    gains = jnp.stack([*first_gains, *second_gains])
    gains = gains + swap(gains)
    if square():
        gains = gains + to_near(gains)
        gains = gains + to_side(gains)
    else:
        gains = lax.psum(gains, "mp")
    gains = sum_line(gains)
    gains = choose(gains[:2], gains[2:])
    ends = jnp.stack([choose(grad_input, got_result), choose(got_input, result)])
    grads = {name: finish(name) for name in ("joined", "out", "gate", "up", "down")}
    return (
        ends[None],
        gains[0][None],
        grads["joined"][:local_width][None],
        grads["joined"][local_width : 2 * local_width][None],
        grads["joined"][2 * local_width :][None],
        grads["out"][None],
        gains[1][None],
        grads["gate"][None],
        grads["up"][None],
        grads["down"][None],
    )


def solution(mesh):
    in_specs = (
        P("section", None, ("dp", "mp"), None),
        P(None, "dp"),
        P("section", None),
        P("section", "mp", None),
        P("section", "mp", None),
        P("section", "mp", None),
        P("section", "mp", None),
        P("section", None),
        P("section", "mp", None),
        P("section", "mp", None),
        P("section", "mp", None),
    )
    out_specs = (
        P("section", None, ("dp", "mp"), None),
        P("section", None),
        P("section", "mp", None),
        P("section", "mp", None),
        P("section", "mp", None),
        P("section", "mp", None),
        P("section", None),
        P("section", "mp", None),
        P("section", "mp", None),
        P("section", "mp", None),
    )
    return jax.shard_map(shards, mesh=mesh, in_specs=in_specs, out_specs=out_specs, check_vma=False)
```
